128 devices in a mesh: row: 16 (over z, y), col: 8 (over x, core).
Axes of the slice: x: 4, y: 4, z: 4, core: 2. Of those that a mesh axis runs over, the one named last changes fastest.
Arguments:
- rhs: float32 [262144, 256], P(('row', 'col')), may hold values from -6 to 6
- block_target: int32 [2048], P(('row', 'col')), may hold values from 0 to 255, as said below
- pivot_inverse: float32 [131072, 1024], P(('row', 'col')), may hold values from -0.25 to 3, as said below
- update_factor: float32 [131072, 1024], P(('row', 'col')), may hold values from -0.1875 to 0.1875
- root_inverse: float32 [16384, 16384], P('row', 'col'), may hold values from -0.25 to 3, as said below
- update_map: int32 [1024], P(('row', 'col')), may hold values from 0 to 127
Outputs:
- front_solution: float32 [131072, 256], P(('row', 'col'))
- root_solution: float32 [16384, 256], P(('row', 'col'))
The draws below stay inside these ranges and needn't reach their ends.
Inputs may be any that keep to these rules, and one draw needn't show every extreme that they name: block_target[g] is e * 16 + s: block g goes to the device of row index e in its own column, slot s there. Each device sends exactly 2 blocks to each of 8 devices of its column and none to the others; every slot of every device is filled exactly once. `pivot_inverse`: each device's block of 1024 rows is lower triangular with its diagonal positive. `root_inverse`: lower triangular with its diagonal positive.
All inputs are finite; a program needn't handle non-finite values.
Results may differ from the reference program's by a relative error of at most 0.000073.
Values sent between devices are 32-bit elements; how exact they have to be, the bound alone decides.
No kernel may reach another device: no remote copies, remote signals or barrier semaphores. Data moves between devices by JAX's collectives and lax.ppermute only.
A program may use at most 192 MiB of HBM per device.

```python
import math
import jax
import jax.numpy as jnp
import numpy as np
from jax import lax

BLK = 128
NRHS = 256
RB_DEV = 16
CAP = 2
HALF = 1024
ROOT = 16384
N_ROW = 16
N_COL = 8
DEVICES = 128


def draw_block_target(key, part):
    base = jax.random.fold_in(key, 7)
    key_offset, key_local, key_slot = jax.random.split(base, 3)
    senders = RB_DEV // CAP
    offsets = jax.vmap(lambda single: jax.random.permutation(single, N_ROW)[:senders])(jax.random.split(key_offset, N_COL))
    ranks = jax.vmap(lambda single: jax.random.permutation(single, RB_DEV))(jax.random.split(key_local, DEVICES))
    shuffles = jax.vmap(lambda single: jax.random.permutation(single, RB_DEV))(jax.random.split(key_slot, DEVICES))
    device = jnp.arange(DEVICES, dtype=jnp.int32)
    row_index = device // N_COL
    col_index = device % N_COL
    group = ranks // CAP
    chosen = jnp.take_along_axis(offsets[col_index], group, axis=1)
    target_row = (row_index[:, None] + chosen) % N_ROW
    receiver = target_row * N_COL + col_index[:, None]
    slot_place = group * CAP + ranks % CAP
    slot_index = shuffles[receiver, slot_place]
    return (target_row * RB_DEV + slot_index).reshape(-1).astype(jnp.int32)


def lower_factor(key, leading, order):
    key_noise, key_diag = jax.random.split(jax.random.fold_in(key, 11))
    noise = jnp.clip(jax.random.normal(key_noise, (leading, order, order), jnp.float32) / math.sqrt(order), -0.25, 0.25)
    diagonal = jax.random.uniform(key_diag, (leading, order, 1), jnp.float32, 1.0, 2.0)
    rows_iota = jnp.arange(order)[:, None]
    cols_iota = jnp.arange(order)[None, :]
    return jnp.where(rows_iota == cols_iota, diagonal, jnp.where(rows_iota > cols_iota, noise, 0.0))


def draw_pivot_inverse(key, part):
    half = BLK * RB_DEV // 2
    return lower_factor(key, DEVICES, half).reshape(DEVICES * half, half)


def draw_root_inverse(key, part):
    return lower_factor(key, 1, ROOT).reshape(ROOT, ROOT)


def plant(array, rng, low, largest):
    shape = array.shape
    place = [jax.random.randint(jax.random.fold_in(rng, axis), (), 0, shape[axis]) for axis in range(len(shape))]
    array = array.at[tuple(place)].set(low)
    longest = shape.index(max(shape))
    place[longest] = (place[longest] + 1) % shape[longest]
    return array.at[tuple(place)].set(largest)


def block_scale(key, dims, shards, smallest, high):
    gain, own = 1.0, jax.random.fold_in(key, 6)
    for dim, blocks in shards:
        draws = jnp.exp(jax.random.uniform(jax.random.fold_in(own, dim), (blocks,), jnp.float32, smallest / len(shards), high / len(shards)))
        gain = gain * jnp.repeat(draws, dims[dim] // blocks).reshape([-1 if axis == dim else 1 for axis in range(len(dims))])
    return gain


def rank_table(amount, skew):
    weights = [(1 << 20) // math.isqrt(standing ** skew) + 1 for standing in range(1, amount + 1)]
    spread = 1 + sum(weights) // (1 << 30)
    return np.cumsum(np.array([max(1, weight // spread) for weight in weights]))


def ranked(own_key, extent, number_of, lean):
    table = rank_table(number_of, lean)
    lot = jax.random.randint(jax.random.fold_in(own_key, 1), extent, 0, int(table[number_of - 1]))
    standing = jnp.searchsorted(jnp.asarray(table, jnp.int32), lot, side="right")
    return jax.random.permutation(jax.random.fold_in(own_key, 2), number_of)[standing].astype(jnp.int32)


def centred(stream_key, dims, deviation, reach, pieces=(), kind=jnp.bfloat16):
    drawn = deviation * jax.random.normal(stream_key, dims, jnp.float32)
    if pieces:
        drawn = drawn * block_scale(stream_key, dims, pieces, -0.22, 0.18)
    return jnp.clip(drawn, -reach, reach).astype(kind)


def setup_inputs(seed: int = 0) -> dict:
    splits = jax.random.split(jax.random.key(seed), 7)
    rhs = centred(splits[0], (DEVICES * RB_DEV * BLK, NRHS), 1.0, 6.0, ((0, 128),), jnp.float32)
    block_target = draw_block_target(jax.random.fold_in(splits[6], 71), 0)
    pivot_inverse = draw_pivot_inverse(jax.random.fold_in(splits[6], 71), 0)
    update_factor = centred(splits[3], (DEVICES * HALF, HALF), HALF ** -0.5, 0.1875, ((0, 128),), jnp.float32)
    root_inverse = draw_root_inverse(jax.random.fold_in(splits[6], 71), 0)
    update_map = plant(ranked(splits[5], (DEVICES * RB_DEV // 2,), DEVICES, 2), jax.random.fold_in(splits[5], 3), 0, DEVICES - 1).astype(jnp.int32)
    return {"rhs": rhs, "block_target": block_target, "pivot_inverse": pivot_inverse, "update_factor": update_factor, "root_inverse": root_inverse, "update_map": update_map}


def reference(rhs, block_target, pivot_inverse, update_factor, root_inverse, update_map):
    count = DEVICES * RB_DEV
    block_index = jnp.arange(count, dtype=jnp.int32)
    column = (block_index // RB_DEV) % N_COL
    where_to = (((block_target // RB_DEV) * N_COL + column) * RB_DEV + block_target % RB_DEV).astype(jnp.int32)
    blocks = rhs.reshape(count, BLK, NRHS)
    fronts = jnp.zeros_like(blocks).at[where_to].set(blocks).reshape(DEVICES, RB_DEV * BLK, NRHS)
    half = BLK * RB_DEV // 2

    def front_step(operands):
        inverse, factor, front = operands
        solved = jnp.dot(inverse, front[:half], precision=lax.Precision.HIGHEST, preferred_element_type=jnp.float32)
        updated = front[half:] - jnp.dot(factor, solved, precision=lax.Precision.HIGHEST, preferred_element_type=jnp.float32)
        return solved, updated

    solved, updated = lax.map(front_step, (pivot_inverse.reshape(DEVICES, half, half), update_factor.reshape(DEVICES, half, half), fronts))
    root_rhs = jnp.zeros((DEVICES, BLK, NRHS), jnp.float32).at[update_map].add(updated.reshape(-1, BLK, NRHS)).reshape(ROOT, NRHS)
    root_solution = jnp.dot(root_inverse, root_rhs, precision=lax.Precision.HIGHEST, preferred_element_type=jnp.float32)
    return solved.reshape(DEVICES * half, NRHS), root_solution
```

```python
import functools

import jax
import jax.numpy as jnp
from jax import lax
from jax.experimental import pallas as pl
from jax.experimental.pallas import tpu as pltpu
from jax.sharding import PartitionSpec as P

BLK = 128
NRHS = 256
RB_DEV = 16
SUB = 8
VMEM_LIMIT = 56 << 20


def split(x):
    high = x.astype(jnp.bfloat16)
    low = (x - high.astype(jnp.float32)).astype(jnp.bfloat16)
    return high, low


def product(a, b_high, b_low):
    a_high, a_low = split(a)
    out = jnp.dot(a_high, b_high, preferred_element_type=jnp.float32)
    out += jnp.dot(a_high, b_low, preferred_element_type=jnp.float32)
    out += jnp.dot(a_low, b_high, preferred_element_type=jnp.float32)
    return out


def exchange(x, axis):
    return lax.all_to_all(x, axis, split_axis=0, concat_axis=0, tiled=True)


def route_kernel(rows, half, index_ref, arrived_ref, send_ref, acc_ref, placed):
    stride = RB_DEV + half
    slots = rows * half

    def place(source, carry):
        for block in range(RB_DEV):
            target = index_ref[source * stride + block]
            owner = target // RB_DEV
            slot = target % RB_DEV
            position = jnp.where(slot < half, owner * half + slot, slots + owner * half + slot - half)
            placed[position] = arrived_ref[source * RB_DEV + block]
        return carry

    lax.fori_loop(0, rows, place, 0)
    acc_ref[...] = jnp.zeros_like(acc_ref)
    send_ref[...] = placed[pl.ds(0, slots)]

    def add(owner, carry):
        for block in range(half):
            root = index_ref[owner * stride + RB_DEV + block]
            acc_ref[root] += placed[slots + owner * half + block]
        return carry

    lax.fori_loop(0, rows, add, 0)


def route(index, arrived, rows, half):
    slots = rows * half
    shape = jax.ShapeDtypeStruct((slots, SUB, NRHS), jnp.float32)
    root_shape = jax.ShapeDtypeStruct((BLK, SUB, NRHS), jnp.float32)
    return pl.pallas_call(
        functools.partial(route_kernel, rows, half),
        out_shape=(shape, root_shape),
        in_specs=[
            pl.BlockSpec(memory_space=pltpu.SMEM),
            pl.BlockSpec(memory_space=pltpu.VMEM),
        ],
        out_specs=(pl.BlockSpec(memory_space=pltpu.VMEM), pl.BlockSpec(memory_space=pltpu.VMEM)),
        scratch_shapes=[pltpu.VMEM((2 * slots, SUB, NRHS), jnp.float32)],
        compiler_params=pltpu.CompilerParams(vmem_limit_bytes=VMEM_LIMIT),
        name="route",
    )(index, arrived)


def front_kernel(tiles, tile, pivot_ref, factor_ref, arrived_ref, solved_ref, update_ref, p_high, p_low, s_high, s_low):
    step = pl.program_id(0)
    blocks = arrived_ref.shape[1]
    per_tile = tile // BLK

    @pl.when(step == 0)
    def _():
        for block in range(blocks):
            high, low = split(arrived_ref[:, block].reshape(BLK, NRHS))
            p_high[pl.ds(block * BLK, BLK)] = high
            p_low[pl.ds(block * BLK, BLK)] = low

    @pl.when(step < tiles)
    def _():
        value = product(pivot_ref[...], p_high[...], p_low[...])
        solved_ref[...] = value
        high, low = split(value)
        start = pl.multiple_of(step * tile, tile)
        s_high[pl.ds(start, tile)] = high
        s_low[pl.ds(start, tile)] = low

    @pl.when(step >= tiles)
    def _():
        value = product(factor_ref[...], s_high[...], s_low[...])
        for block in range(per_tile):
            update_ref[:, (step - tiles) * per_tile + block] = value[block * BLK : (block + 1) * BLK].reshape(
                update_ref.shape[0], SUB, NRHS
            )


def front(arrived, pivot_inverse, update_factor):
    rows, half = arrived.shape[:2]
    order = half * BLK
    tile = 256
    tiles = order // tile
    return pl.pallas_call(
        functools.partial(front_kernel, tiles, tile),
        grid=(2 * tiles,),
        out_shape=(
            jax.ShapeDtypeStruct((order, NRHS), jnp.float32),
            jax.ShapeDtypeStruct((rows, half, SUB, NRHS), jnp.float32),
        ),
        in_specs=[
            pl.BlockSpec((tile, order), lambda i: (jnp.minimum(i, tiles - 1), 0)),
            pl.BlockSpec((tile, order), lambda i: (jnp.maximum(i - tiles, 0), 0)),
            pl.BlockSpec((rows, half, SUB, NRHS), lambda i: (0, 0, 0, 0)),
        ],
        out_specs=(
            pl.BlockSpec((tile, NRHS), lambda i: (jnp.minimum(i, tiles - 1), 0)),
            pl.BlockSpec((rows, half, SUB, NRHS), lambda i: (0, 0, 0, 0)),
        ),
        scratch_shapes=[pltpu.VMEM((order, NRHS), jnp.bfloat16)] * 4,
        compiler_params=pltpu.CompilerParams(vmem_limit_bytes=VMEM_LIMIT),
        name="front",
    )(pivot_inverse, update_factor, arrived)


def subtract_kernel(rows, half, index_ref, arrived_ref, start_ref, acc_ref):
    stride = RB_DEV + half
    acc_ref[...] = start_ref[...]

    def add(owner, carry):
        for block in range(half):
            root = index_ref[owner * stride + RB_DEV + block]
            acc_ref[root] -= arrived_ref[owner * half + block]
        return carry

    lax.fori_loop(0, rows, add, 0)


def subtract(index, arrived, start, rows, half):
    return pl.pallas_call(
        functools.partial(subtract_kernel, rows, half),
        out_shape=jax.ShapeDtypeStruct(start.shape, jnp.float32),
        in_specs=[
            pl.BlockSpec(memory_space=pltpu.SMEM),
            pl.BlockSpec(memory_space=pltpu.VMEM),
            pl.BlockSpec(memory_space=pltpu.VMEM),
        ],
        out_specs=pl.BlockSpec(memory_space=pltpu.VMEM),
        compiler_params=pltpu.CompilerParams(vmem_limit_bytes=VMEM_LIMIT),
        name="subtract",
    )(index, arrived, start)


def root_kernel(gathered_ref, inverse_ref, out_ref, r_high, r_low):
    @pl.when(pl.program_id(0) == 0)
    def _():
        for block in range(gathered_ref.shape[1]):
            high, low = split(gathered_ref[:, block].reshape(BLK, NRHS))
            r_high[pl.ds(block * BLK, BLK)] = high
            r_low[pl.ds(block * BLK, BLK)] = low

    out_ref[...] = product(inverse_ref[...], r_high[...], r_low[...])


def root(gathered, root_inverse):
    height, depth = root_inverse.shape
    tile = 256
    return pl.pallas_call(
        root_kernel,
        grid=(height // tile,),
        out_shape=jax.ShapeDtypeStruct((height, NRHS), jnp.float32),
        in_specs=[
            pl.BlockSpec(gathered.shape, lambda i: (0, 0, 0, 0)),
            pl.BlockSpec((tile, depth), lambda i: (i, 0)),
        ],
        out_specs=pl.BlockSpec((tile, NRHS), lambda i: (i, 0)),
        scratch_shapes=[pltpu.VMEM((depth, NRHS), jnp.bfloat16)] * 2,
        compiler_params=pltpu.CompilerParams(vmem_limit_bytes=VMEM_LIMIT),
        name="root",
    )(gathered, root_inverse)


def shards(rhs, block_target, pivot_inverse, update_factor, root_inverse, update_map):
    rows = lax.axis_size("row")
    cols = lax.axis_size("col")
    half = update_map.shape[0]
    index = lax.all_gather(jnp.concatenate([block_target, update_map]), "row", axis=0, tiled=True)
    sliced = rhs.reshape(RB_DEV, rows, SUB, NRHS).transpose(1, 0, 2, 3)
    arrived = exchange(sliced, "row").reshape(rows * RB_DEV, SUB, NRHS)
    send, direct = route(index, arrived, rows, half)
    pivot = exchange(send.reshape(rows, half, SUB, NRHS), "row")
    solved, update = front(pivot, pivot_inverse, update_factor)
    returned = exchange(update, "row").reshape(rows * half, SUB, NRHS)
    partial_root = subtract(index, returned, direct, rows, half)
    per_col = BLK // cols
    piece = jnp.sum(exchange(partial_root.reshape(cols, per_col, SUB, NRHS), "col"), axis=0)
    gathered = exchange(jnp.broadcast_to(piece[None], (rows,) + piece.shape), "row")
    partial_value = root(gathered, root_inverse)
    root_solution = jnp.sum(exchange(partial_value.reshape(cols, -1, NRHS), "col"), axis=0)
    return (solved, root_solution)


def solution(mesh):
    return jax.shard_map(
        shards,
        mesh=mesh,
        in_specs=(
            P(("row", "col"), None),
            P(("row", "col")),
            P(("row", "col"), None),
            P(("row", "col"), None),
            P("row", "col"),
            P(("row", "col")),
        ),
        out_specs=(P(("row", "col"), None), P(("row", "col"), None)),
        check_vma=False,
    )
```

```python
import functools

import jax
import jax.numpy as jnp
from jax import lax
from jax.experimental import pallas as pl
from jax.experimental.pallas import tpu as pltpu
from jax.sharding import PartitionSpec as P

BLK = 128
NRHS = 256
RB_DEV = 16
SUB = 8
LANES = 128
CORES = 2
VMEM_LIMIT = 8 << 20
TILE = 256
VMEM = pl.BlockSpec(memory_space=pltpu.VMEM)
SMEM = pl.BlockSpec(memory_space=pltpu.SMEM)
ANY = pl.BlockSpec(memory_space=pl.ANY)
PARAMS = pltpu.CompilerParams(vmem_limit_bytes=VMEM_LIMIT)


def f32(*shape):
    return jax.ShapeDtypeStruct(shape, jnp.float32)


def far(x):
    return pltpu.with_memory_space_constraint(x, pltpu.HBM)


def split(x):
    high = x.astype(jnp.bfloat16)
    low = (x - high.astype(jnp.float32)).astype(jnp.bfloat16)
    return high, low


def product(a_high, a_low, b_high, b_low):
    out = jnp.dot(a_high, b_high, preferred_element_type=jnp.float32)
    out += jnp.dot(a_high, b_low, preferred_element_type=jnp.float32)
    out += jnp.dot(a_low, b_high, preferred_element_type=jnp.float32)
    return out


def exchange(x, axis):
    return lax.all_to_all(x, axis, split_axis=0, concat_axis=0, tiled=True)


def pack_kernel(rows, half, target_ref, map_ref, rhs_ref, out_ref, targets, roots, sems, table_sems):
    tables = [
        pltpu.make_async_copy(target_ref, targets, table_sems.at[0]),
        pltpu.make_async_copy(map_ref, roots, table_sems.at[1]),
    ]
    copies = [
        pltpu.make_async_copy(rhs_ref.at[block], out_ref.at[:, block], sems.at[block]) for block in range(RB_DEV)
    ]
    for copy in tables + copies:
        copy.start()
    for copy in tables:
        copy.wait()
    lane = lax.broadcasted_iota(jnp.int32, (SUB, NRHS), 1)
    words = jnp.zeros((SUB, NRHS), jnp.int32)
    for i in range(RB_DEV):
        words = jnp.where(lane == i, targets[i], words)
    for i in range(half):
        words = jnp.where(lane == RB_DEV + i, roots[i], words)
    words = words.astype(jnp.float32)
    for peer in range(rows):
        out_ref[peer, RB_DEV] = words
    for copy in copies:
        copy.wait()


def pack(rhs, block_target, update_map, rows):
    half = update_map.shape[0]
    return pl.pallas_call(
        functools.partial(pack_kernel, rows, half),
        out_shape=f32(rows, RB_DEV + 1, SUB, NRHS),
        in_specs=[ANY] * 3,
        out_specs=VMEM,
        scratch_shapes=[
            pltpu.SMEM((RB_DEV,), jnp.int32),
            pltpu.SMEM((half,), jnp.int32),
            pltpu.SemaphoreType.DMA((RB_DEV,)),
            pltpu.SemaphoreType.DMA((2,)),
        ],
        compiler_params=PARAMS,
        name="pack",
    )(far(block_target), far(update_map), far(rhs.reshape(RB_DEV, rows, SUB, NRHS)))


def relative(root, per_col, chips):
    me = lax.axis_index("col")
    col = root // per_col
    distance = (col // CORES - me // CORES + chips) % chips
    other = (col + me) % CORES
    return (other * chips + distance) * per_col + root % per_col


def route_kernel(rows, half, chips, arrived_ref, send_ref, acc_ref, root_ref, words, table, sem):
    slots = rows * half
    received = arrived_ref[:, RB_DEV, 0, :LANES].astype(jnp.int32)
    lane = lax.broadcasted_iota(jnp.int32, received.shape, 1)
    owner = received // RB_DEV
    slot = received % RB_DEV
    entry = owner * half + slot + jnp.where(slot < half, 0, slots - half)
    words[...] = jnp.where(lane < RB_DEV, entry, slots + relative(received, BLK // (CORES * chips), chips))
    copy = pltpu.make_async_copy(words, table, sem)
    copy.start()
    acc_ref[...] = jnp.zeros_like(acc_ref)
    copy.wait()

    def place(source, carry):
        for block in range(RB_DEV):
            where = table[source, block]
            update = where >= slots
            index = lax.bitwise_and(where, slots - 1)
            root = table[lax.shift_right_logical(index, half.bit_length() - 1), RB_DEV + lax.bitwise_and(index, half - 1)]
            position = jnp.where(update, root, index)
            acc_ref[position] += arrived_ref[source, block]
        return carry

    lax.fori_loop(0, rows, place, 0)
    send_ref[...] = acc_ref[pl.ds(0, slots)]
    for row in range(rows):
        for block in range(half):
            root_ref[row * half + block] = table[row, RB_DEV + block]


def route(arrived, rows, half, chips):
    slots = rows * half
    return pl.pallas_call(
        functools.partial(route_kernel, rows, half, chips),
        out_shape=(
            f32(slots, SUB, NRHS),
            f32(slots + BLK, SUB, NRHS),
            jax.ShapeDtypeStruct((slots,), jnp.int32),
        ),
        in_specs=[VMEM],
        out_specs=(VMEM, VMEM, SMEM),
        scratch_shapes=[
            pltpu.VMEM((rows, LANES), jnp.int32),
            pltpu.SMEM((rows, LANES), jnp.int32),
            pltpu.SemaphoreType.DMA,
        ],
        compiler_params=PARAMS,
        name="route",
    )(arrived)


def split_into(value, high_ref, low_ref, start):
    high, low = split(value)
    high_ref[pl.ds(start, value.shape[0])] = high
    low_ref[pl.ds(start, value.shape[0])] = low


def front_kernel(arrived_ref, pivot_ref, factor_ref, solved_ref, update_ref, p_high, p_low, s_high, s_low):
    rows, blocks = arrived_ref.shape[:2]
    order = blocks * BLK
    for block in range(blocks):
        split_into(arrived_ref[:, block].reshape(BLK, NRHS), p_high, p_low, block * BLK)
    for start in range(0, order, TILE):
        here, depth = pl.ds(start, TILE), pl.ds(0, start + TILE)
        value = product(*split(pivot_ref[here, depth]), p_high[depth], p_low[depth])
        solved_ref[here] = value
        split_into(value, s_high, s_low, start)
    for start in range(0, order, TILE):
        value = product(*split(factor_ref[pl.ds(start, TILE)]), s_high[...], s_low[...])
        for block in range(TILE // BLK):
            part = value[block * BLK : (block + 1) * BLK]
            update_ref[:, start // BLK + block] = part.reshape(rows, SUB, NRHS)


def front(arrived, pivot_inverse, update_factor):
    rows, half = arrived.shape[:2]
    order = half * BLK
    return pl.pallas_call(
        front_kernel,
        out_shape=(f32(order, NRHS), f32(rows, half, SUB, NRHS)),
        in_specs=[VMEM] * 3,
        out_specs=(VMEM, VMEM),
        scratch_shapes=[pltpu.VMEM((order, NRHS), jnp.bfloat16)] * 4,
        compiler_params=PARAMS,
        name="front",
    )(arrived, pivot_inverse, update_factor)


def subtract_kernel(rows, half, root_ref, arrived_ref, start_ref, mine_ref, other_ref, acc):
    slots = rows * half
    acc[...] = start_ref[pl.ds(slots, BLK)]

    def add(owner, carry):
        for block in range(half):
            acc[root_ref[owner * half + block] - slots] -= arrived_ref[owner, block]
        return carry

    lax.fori_loop(0, rows, add, 0)
    mine_ref[...] = acc[pl.ds(0, BLK // CORES)].reshape(mine_ref.shape)
    other_ref[...] = acc[pl.ds(BLK // CORES, BLK // CORES)].reshape(mine_ref.shape)


def subtract(root, arrived, start, chips):
    rows, half = arrived.shape[:2]
    out = f32(chips, BLK // (CORES * chips), SUB, NRHS)
    return pl.pallas_call(
        functools.partial(subtract_kernel, rows, half),
        out_shape=(out, out),
        in_specs=[SMEM, VMEM, VMEM],
        out_specs=(VMEM, VMEM),
        scratch_shapes=[pltpu.VMEM((BLK, SUB, NRHS), jnp.float32)],
        compiler_params=PARAMS,
        name="subtract",
    )(root, arrived, start)


def root_kernel(chips, gathered_ref, inverse_ref, mine_ref, other_ref, r_high, r_low):
    for block in range(gathered_ref.shape[1]):
        split_into(gathered_ref[:, block].reshape(BLK, NRHS), r_high, r_low, block * BLK)
    me = lax.axis_index("col")
    height = mine_ref.shape[1]
    for distance in range(chips):
        chip = (me // CORES + distance) % chips
        strip = inverse_ref[pl.ds(pl.multiple_of(chip * CORES * height, CORES * height), CORES * height)]
        value = product(*split(strip), r_high[...], r_low[...])
        first, second = value[:height], value[height:]
        even = me % CORES == 0
        mine_ref[distance] = jnp.where(even, first, second)
        other_ref[distance] = jnp.where(even, second, first)


def root(gathered, root_inverse, chips):
    height, depth = root_inverse.shape
    out = f32(chips, height // (CORES * chips), NRHS)
    return pl.pallas_call(
        functools.partial(root_kernel, chips),
        out_shape=(out, out),
        in_specs=[VMEM] * 2,
        out_specs=(VMEM, VMEM),
        scratch_shapes=[pltpu.VMEM((depth, NRHS), jnp.bfloat16)] * 2,
        compiler_params=PARAMS,
        name="root",
    )(gathered, root_inverse)


def reduce_cols(mine, other, cols):
    chips = cols // CORES
    sibling = lax.ppermute(other, "col", [(c, c ^ 1) for c in range(cols)])
    total = mine[0] + sibling[0]
    parts = [
        lax.ppermute(
            mine[distance] + sibling[distance], "col", [(c, (c + CORES * distance) % cols) for c in range(cols)]
        )
        for distance in range(1, chips)
    ]
    for part in parts:
        total = total + part
    return total


def shards(rhs, block_target, pivot_inverse, update_factor, root_inverse, update_map):
    rows = lax.axis_size("row")
    cols = lax.axis_size("col")
    chips = cols // CORES
    half = update_map.shape[0]
    arrived = exchange(pack(rhs, block_target, update_map, rows), "row")
    send, direct, root_index = route(arrived, rows, half, chips)
    pivot = exchange(send.reshape(rows, half, SUB, NRHS), "row")
    solved, update = front(pivot, pivot_inverse, update_factor)
    returned = exchange(update, "row")
    piece = reduce_cols(*subtract(root_index, returned, direct, chips), cols)
    gathered = exchange(jnp.broadcast_to(piece[None], (rows,) + piece.shape), "row")
    root_solution = reduce_cols(*root(gathered, root_inverse, chips), cols)
    return (solved, root_solution)


def solution(mesh):
    return jax.shard_map(
        shards,
        mesh=mesh,
        in_specs=(
            P(("row", "col"), None),
            P(("row", "col")),
            P(("row", "col"), None),
            P(("row", "col"), None),
            P("row", "col"),
            P(("row", "col")),
        ),
        out_specs=(P(("row", "col"), None), P(("row", "col"), None)),
        check_vma=False,
    )
```

```python
import functools

import jax
import jax.numpy as jnp
from jax import lax
from jax.experimental import pallas as pl
from jax.experimental.pallas import tpu as pltpu
from jax.sharding import PartitionSpec as P

BLK = 128
NRHS = 256
RB_DEV = 16
SUB = 8
LANES = 128
TILES = NRHS // LANES
CORES = 2
VMEM_LIMIT = 8 << 20
TILE = 256
VMEM = pl.BlockSpec(memory_space=pltpu.VMEM)
SMEM = pl.BlockSpec(memory_space=pltpu.SMEM)
ANY = pl.BlockSpec(memory_space=pl.ANY)
PARAMS = pltpu.CompilerParams(vmem_limit_bytes=VMEM_LIMIT)


def f32(*shape):
    return jax.ShapeDtypeStruct(shape, jnp.float32)


def far(x):
    return pltpu.with_memory_space_constraint(x, pltpu.HBM)


def split(x):
    high = x.astype(jnp.bfloat16)
    low = (x - high.astype(jnp.float32)).astype(jnp.bfloat16)
    return high, low


def product(a_high, a_low, b_high, b_low):
    out = jnp.dot(a_high, b_high, preferred_element_type=jnp.float32)
    out += jnp.dot(a_high, b_low, preferred_element_type=jnp.float32)
    out += jnp.dot(a_low, b_high, preferred_element_type=jnp.float32)
    return out


def exchange(x, axis):
    return lax.all_to_all(x, axis, split_axis=0, concat_axis=0, tiled=True)


def pack_kernel(rows, half, target_ref, map_ref, rhs_ref, out_ref, targets, roots, sems, table_sems):
    tables = [
        pltpu.make_async_copy(target_ref, targets, table_sems.at[0]),
        pltpu.make_async_copy(map_ref, roots, table_sems.at[1]),
    ]
    copies = [
        pltpu.make_async_copy(
            rhs_ref.at[block, :, :, pl.ds(lane * LANES, LANES)],
            out_ref.at[:, block * TILES + lane],
            sems.at[block * TILES + lane],
        )
        for block in range(RB_DEV)
        for lane in range(TILES)
    ]
    for copy in tables + copies:
        copy.start()
    for copy in tables:
        copy.wait()
    lane = lax.broadcasted_iota(jnp.int32, (SUB, LANES), 1)
    words = jnp.zeros((SUB, LANES), jnp.int32)
    for i in range(RB_DEV):
        words = jnp.where(lane == i, targets[i], words)
    for i in range(half):
        words = jnp.where(lane == RB_DEV + i, roots[i], words)
    words = words.astype(jnp.float32)
    for peer in range(rows):
        out_ref[peer, RB_DEV * TILES] = words
    for copy in copies:
        copy.wait()


def pack(rhs, block_target, update_map, rows):
    half = update_map.shape[0]
    return pl.pallas_call(
        functools.partial(pack_kernel, rows, half),
        out_shape=f32(rows, RB_DEV * TILES + 1, SUB, LANES),
        in_specs=[ANY] * 3,
        out_specs=VMEM,
        scratch_shapes=[
            pltpu.SMEM((RB_DEV,), jnp.int32),
            pltpu.SMEM((half,), jnp.int32),
            pltpu.SemaphoreType.DMA((RB_DEV * TILES,)),
            pltpu.SemaphoreType.DMA((2,)),
        ],
        compiler_params=PARAMS,
        name="pack",
    )(far(block_target), far(update_map), far(rhs.reshape(RB_DEV, rows, SUB, NRHS)))


def relative(root, per_col, chips):
    me = lax.axis_index("col")
    col = root // per_col
    distance = (col // CORES - me // CORES + chips) % chips
    other = (col + me) % CORES
    return (other * chips + distance) * per_col + root % per_col


def route_kernel(rows, half, chips, arrived_ref, send_ref, acc_ref, words, table, sem):
    slots = rows * half
    received = arrived_ref[:, RB_DEV * TILES, 0].astype(jnp.int32)
    lane = lax.broadcasted_iota(jnp.int32, received.shape, 1)
    owner = received // RB_DEV
    slot = received % RB_DEV
    entry = owner * half + slot + jnp.where(slot < half, 0, slots - half)
    words[...] = jnp.where(lane < RB_DEV, entry, slots + relative(received, BLK // (CORES * chips), chips))
    copy = pltpu.make_async_copy(words, table, sem)
    copy.start()
    acc_ref[...] = jnp.zeros_like(acc_ref)
    copy.wait()

    def place(source, carry):
        for block in range(RB_DEV):
            where = table[source, block]
            update = where >= slots
            index = lax.bitwise_and(where, slots - 1)
            root = table[lax.shift_right_logical(index, half.bit_length() - 1), RB_DEV + lax.bitwise_and(index, half - 1)]
            position = jnp.where(update, root, index)
            acc_ref[position] += arrived_ref[source, pl.ds(block * TILES, TILES)]
        return carry

    lax.fori_loop(0, rows, place, 0)
    send_ref[...] = acc_ref[pl.ds(0, slots)]


def route(arrived, rows, half, chips):
    slots = rows * half
    return pl.pallas_call(
        functools.partial(route_kernel, rows, half, chips),
        out_shape=(
            f32(slots, TILES, SUB, LANES),
            f32(slots + BLK, TILES, SUB, LANES),
            jax.ShapeDtypeStruct((rows, LANES), jnp.int32),
        ),
        in_specs=[VMEM],
        out_specs=(VMEM, VMEM, VMEM),
        scratch_shapes=[
            pltpu.SMEM((rows, LANES), jnp.int32),
            pltpu.SemaphoreType.DMA,
        ],
        compiler_params=PARAMS,
        name="route",
    )(arrived)


def split_into(value, high_ref, low_ref, start, lane=0):
    high, low = split(value)
    here = (pl.ds(start, value.shape[0]), pl.ds(lane * LANES, value.shape[1]))
    high_ref[here] = high
    low_ref[here] = low


def join_slices(slices_ref, high_ref, low_ref):
    for block in range(slices_ref.shape[1]):
        for lane in range(TILES):
            split_into(slices_ref[:, block, lane].reshape(BLK, LANES), high_ref, low_ref, block * BLK, lane)


def front_kernel(arrived_ref, pivot_ref, factor_ref, solved_ref, update_ref, p_high, p_low, s_high, s_low):
    rows, blocks = arrived_ref.shape[:2]
    order = blocks * BLK
    join_slices(arrived_ref, p_high, p_low)
    for start in range(0, order, TILE):
        here, depth = pl.ds(start, TILE), pl.ds(0, start + TILE)
        value = product(*split(pivot_ref[here, depth]), p_high[depth], p_low[depth])
        solved_ref[here] = value
        split_into(value, s_high, s_low, start)
    for start in range(0, order, TILE):
        value = product(*split(factor_ref[pl.ds(start, TILE)]), s_high[...], s_low[...])
        for block in range(TILE // BLK):
            for lane in range(TILES):
                part = value[block * BLK : (block + 1) * BLK, lane * LANES : (lane + 1) * LANES]
                update_ref[:, start // BLK + block, lane] = part.reshape(rows, SUB, LANES)


def front(arrived, pivot_inverse, update_factor):
    rows, half = arrived.shape[:2]
    order = half * BLK
    return pl.pallas_call(
        front_kernel,
        out_shape=(f32(order, NRHS), f32(rows, half, TILES, SUB, LANES)),
        in_specs=[VMEM] * 3,
        out_specs=(VMEM, VMEM),
        scratch_shapes=[pltpu.VMEM((order, NRHS), jnp.bfloat16)] * 4,
        compiler_params=PARAMS,
        name="front",
    )(arrived, pivot_inverse, update_factor)


def subtract_kernel(rows, half, words_ref, arrived_ref, start_ref, mine_ref, other_ref, acc):
    slots = rows * half
    acc[...] = start_ref[pl.ds(slots, BLK)]

    def add(owner, carry):
        for block in range(half):
            acc[words_ref[owner, RB_DEV + block] - slots] -= arrived_ref[owner, block]
        return carry

    lax.fori_loop(0, rows, add, 0)
    mine_ref[...] = acc[pl.ds(0, BLK // CORES)].reshape(mine_ref.shape)
    other_ref[...] = acc[pl.ds(BLK // CORES, BLK // CORES)].reshape(mine_ref.shape)


def subtract(words, arrived, start, chips):
    rows, half = arrived.shape[:2]
    out = f32(chips, BLK // (CORES * chips), TILES, SUB, LANES)
    return pl.pallas_call(
        functools.partial(subtract_kernel, rows, half),
        out_shape=(out, out),
        in_specs=[SMEM, VMEM, VMEM],
        out_specs=(VMEM, VMEM),
        scratch_shapes=[pltpu.VMEM((BLK, TILES, SUB, LANES), jnp.float32)],
        compiler_params=PARAMS,
        name="subtract",
    )(words, arrived, start)


def root_rows(swap, inverse_ref, r_high, r_low, out_ref):
    me = lax.axis_index("col")
    chips, height = out_ref.shape[:2]
    for distance in range(chips):
        base = ((me // CORES + distance) % chips * CORES + (me + swap) % CORES) * height
        strip = inverse_ref[pl.ds(pl.multiple_of(base, height), height)]
        out_ref[distance] = product(*split(strip), r_high[...], r_low[...])


def root_other_kernel(gathered_ref, inverse_ref, other_ref, high_ref, low_ref):
    join_slices(gathered_ref, high_ref, low_ref)
    root_rows(1, inverse_ref, high_ref, low_ref, other_ref)


def root_mine_kernel(high_ref, low_ref, inverse_ref, mine_ref):
    root_rows(0, inverse_ref, high_ref, low_ref, mine_ref)


def root(gathered, root_inverse, chips):
    height, depth = root_inverse.shape
    out = f32(chips, height // (CORES * chips), NRHS)
    half = jax.ShapeDtypeStruct((depth, NRHS), jnp.bfloat16)
    cost = pl.CostEstimate(flops=3 * height * depth * NRHS, transcendentals=0, bytes_accessed=2 * height * depth)
    other, high, low = pl.pallas_call(
        root_other_kernel,
        out_shape=(out, half, half),
        in_specs=[VMEM] * 2,
        out_specs=(VMEM,) * 3,
        compiler_params=PARAMS,
        cost_estimate=cost,
        name="root_other",
    )(gathered, root_inverse)
    mine = pl.pallas_call(
        root_mine_kernel,
        out_shape=out,
        in_specs=[VMEM] * 3,
        out_specs=VMEM,
        compiler_params=PARAMS,
        cost_estimate=cost,
        name="root_mine",
    )(high, low, root_inverse)
    return mine, other


def reduce_cols(mine, other, cols):
    chips = cols // CORES
    sibling = lax.ppermute(other, "col", [(c, c ^ 1) for c in range(cols)])
    total = mine[0] + sibling[0]
    parts = [
        lax.ppermute(
            mine[distance] + sibling[distance], "col", [(c, (c + CORES * distance) % cols) for c in range(cols)]
        )
        for distance in range(1, chips)
    ]
    for part in parts:
        total = total + part
    return total


def shards(rhs, block_target, pivot_inverse, update_factor, root_inverse, update_map):
    rows = lax.axis_size("row")
    cols = lax.axis_size("col")
    chips = cols // CORES
    half = update_map.shape[0]
    arrived = exchange(pack(rhs, block_target, update_map, rows), "row")
    send, direct, words = route(arrived, rows, half, chips)
    pivot = exchange(send.reshape(rows, half, TILES, SUB, LANES), "row")
    solved, update = front(pivot, pivot_inverse, update_factor)
    returned = exchange(update, "row")
    piece = reduce_cols(*subtract(words, returned, direct, chips), cols)
    gathered = exchange(jnp.broadcast_to(piece[None], (rows,) + piece.shape), "row")
    root_solution = reduce_cols(*root(gathered, root_inverse, chips), cols)
    return (solved, root_solution)


def solution(mesh):
    return jax.shard_map(
        shards,
        mesh=mesh,
        in_specs=(
            P(("row", "col"), None),
            P(("row", "col")),
            P(("row", "col"), None),
            P(("row", "col"), None),
            P("row", "col"),
            P(("row", "col")),
        ),
        out_specs=(P(("row", "col"), None), P(("row", "col"), None)),
        check_vma=False,
    )
```

```python
import functools
import math

import jax
import jax.numpy as jnp
from jax import lax
from jax.experimental import pallas as pl
from jax.experimental.pallas import tpu as pltpu
from jax.sharding import PartitionSpec as P

BLK = 128
NRHS = 256
RB_DEV = 16
SUB = 8
LANES = 128
TILES = NRHS // LANES
CORES = 2
VMEM_LIMIT = 8 << 20
TILE = 256
VMEM = pl.BlockSpec(memory_space=pltpu.VMEM)
SMEM = pl.BlockSpec(memory_space=pltpu.SMEM)
ANY = pl.BlockSpec(memory_space=pl.ANY)
PARAMS = pltpu.CompilerParams(vmem_limit_bytes=VMEM_LIMIT)


def f32(*shape):
    return jax.ShapeDtypeStruct(shape, jnp.float32)


def far(x):
    return pltpu.with_memory_space_constraint(x, pltpu.HBM)


def split(x):
    high = x.astype(jnp.bfloat16)
    low = (x - high.astype(jnp.float32)).astype(jnp.bfloat16)
    return high, low


def product(a_high, a_low, b_high, b_low):
    out = jnp.dot(a_high, b_high, preferred_element_type=jnp.float32)
    out += jnp.dot(a_high, b_low, preferred_element_type=jnp.float32)
    out += jnp.dot(a_low, b_high, preferred_element_type=jnp.float32)
    return out


def exchange(x, axis):
    return lax.all_to_all(x, axis, split_axis=0, concat_axis=0, tiled=True)


def pack_kernel(rows, half, target_ref, map_ref, rhs_ref, out_ref, targets, roots, sems, table_sems):
    tables = [
        pltpu.make_async_copy(target_ref, targets, table_sems.at[0]),
        pltpu.make_async_copy(map_ref, roots, table_sems.at[1]),
    ]
    copies = [
        pltpu.make_async_copy(
            rhs_ref.at[block, :, :, pl.ds(lane * LANES, LANES)],
            out_ref.at[:, block * TILES + lane],
            sems.at[block * TILES + lane],
        )
        for block in range(RB_DEV)
        for lane in range(TILES)
    ]
    for copy in tables + copies:
        copy.start()
    for copy in tables:
        copy.wait()
    lane = lax.broadcasted_iota(jnp.int32, (SUB, LANES), 1)
    words = jnp.zeros((SUB, LANES), jnp.int32)
    for i in range(RB_DEV):
        words = jnp.where(lane == i, targets[i], words)
    for i in range(half):
        words = jnp.where(lane == RB_DEV + i, roots[i], words)
    words = words.astype(jnp.float32)
    for peer in range(rows):
        out_ref[peer, RB_DEV * TILES] = words
    for copy in copies:
        copy.wait()


def pack(rhs, block_target, update_map, rows):
    half = update_map.shape[0]
    return pl.pallas_call(
        functools.partial(pack_kernel, rows, half),
        out_shape=f32(rows, RB_DEV * TILES + 1, SUB, LANES),
        in_specs=[ANY] * 3,
        out_specs=VMEM,
        scratch_shapes=[
            pltpu.SMEM((RB_DEV,), jnp.int32),
            pltpu.SMEM((half,), jnp.int32),
            pltpu.SemaphoreType.DMA((RB_DEV * TILES,)),
            pltpu.SemaphoreType.DMA((2,)),
        ],
        compiler_params=PARAMS,
        name="pack",
    )(far(block_target), far(update_map), far(rhs.reshape(RB_DEV, rows, SUB, NRHS)))


def relative(root, per_col, chips):
    me = lax.axis_index("col")
    col = root // per_col
    distance = (col // CORES - me // CORES + chips) % chips
    other = (col + me) % CORES
    return (other * chips + distance) * per_col + root % per_col


def route_kernel(rows, half, chips, arrived_ref, send_ref, acc_ref, words, table, sem):
    slots = rows * half
    received = arrived_ref[:, RB_DEV * TILES, 0].astype(jnp.int32)
    lane = lax.broadcasted_iota(jnp.int32, received.shape, 1)
    owner = received // RB_DEV
    slot = received % RB_DEV
    entry = owner * half + slot + jnp.where(slot < half, 0, slots - half)
    words[...] = jnp.where(lane < RB_DEV, entry, slots + relative(received, BLK // (CORES * chips), chips))
    copy = pltpu.make_async_copy(words, table, sem)
    copy.start()
    acc_ref[...] = jnp.zeros_like(acc_ref)
    copy.wait()

    def place(source, carry):
        for block in range(RB_DEV):
            where = table[source, block]
            update = where >= slots
            index = lax.bitwise_and(where, slots - 1)
            root = table[lax.shift_right_logical(index, half.bit_length() - 1), RB_DEV + lax.bitwise_and(index, half - 1)]
            position = jnp.where(update, root, index)
            acc_ref[position] += arrived_ref[source, pl.ds(block * TILES, TILES)]
        return carry

    lax.fori_loop(0, rows, place, 0)
    send_ref[...] = acc_ref[pl.ds(0, slots)]


def route(arrived, rows, half, chips):
    slots = rows * half
    return pl.pallas_call(
        functools.partial(route_kernel, rows, half, chips),
        out_shape=(
            f32(slots, TILES, SUB, LANES),
            f32(slots + BLK, TILES, SUB, LANES),
            jax.ShapeDtypeStruct((rows, LANES), jnp.int32),
        ),
        in_specs=[VMEM],
        out_specs=(VMEM, VMEM, VMEM),
        scratch_shapes=[
            pltpu.SMEM((rows, LANES), jnp.int32),
            pltpu.SemaphoreType.DMA,
        ],
        compiler_params=PARAMS,
        name="route",
    )(arrived)


def split_into(value, high_ref, low_ref, start, lane=0):
    high, low = split(value)
    here = (pl.ds(start, value.shape[0]), pl.ds(lane * LANES, value.shape[1]))
    high_ref[here] = high
    low_ref[here] = low


def join_slices(slices_ref, high_ref, low_ref):
    for block in range(slices_ref.shape[1]):
        for lane in range(TILES):
            split_into(slices_ref[:, block, lane].reshape(BLK, LANES), high_ref, low_ref, block * BLK, lane)


def front_kernel(arrived_ref, pivot_ref, factor_ref, solved_ref, update_ref, p_high, p_low, s_high, s_low):
    rows, blocks = arrived_ref.shape[:2]
    order = blocks * BLK
    join_slices(arrived_ref, p_high, p_low)
    for start in range(0, order, TILE):
        here, depth = pl.ds(start, TILE), pl.ds(0, start + TILE)
        value = product(*split(pivot_ref[here, depth]), p_high[depth], p_low[depth])
        solved_ref[here] = value
        split_into(value, s_high, s_low, start)
    for start in range(0, order, TILE):
        value = product(*split(factor_ref[pl.ds(start, TILE)]), s_high[...], s_low[...])
        for block in range(TILE // BLK):
            for lane in range(TILES):
                part = value[block * BLK : (block + 1) * BLK, lane * LANES : (lane + 1) * LANES]
                update_ref[:, start // BLK + block, lane] = part.reshape(rows, SUB, LANES)


def front(arrived, pivot_inverse, update_factor):
    rows, half = arrived.shape[:2]
    order = half * BLK
    return pl.pallas_call(
        front_kernel,
        out_shape=(f32(order, NRHS), f32(rows, half, TILES, SUB, LANES)),
        in_specs=[VMEM] * 3,
        out_specs=(VMEM, VMEM),
        scratch_shapes=[pltpu.VMEM((order, NRHS), jnp.bfloat16)] * 4,
        compiler_params=PARAMS,
        name="front",
    )(arrived, pivot_inverse, update_factor)


def subtract_kernel(rows, half, words_ref, arrived_ref, start_ref, mine_ref, other_ref, acc):
    slots = rows * half
    acc[...] = start_ref[pl.ds(slots, BLK)]

    def add(owner, carry):
        for block in range(half):
            acc[words_ref[owner, RB_DEV + block] - slots] -= arrived_ref[owner, block]
        return carry

    lax.fori_loop(0, rows, add, 0)
    mine_ref[...] = acc[pl.ds(0, BLK // CORES)].reshape(mine_ref.shape)
    other_ref[...] = acc[pl.ds(BLK // CORES, BLK // CORES)].reshape(mine_ref.shape)


def subtract(words, arrived, start, chips):
    rows, half = arrived.shape[:2]
    out = f32(chips, BLK // (CORES * chips), TILES, SUB, LANES)
    return pl.pallas_call(
        functools.partial(subtract_kernel, rows, half),
        out_shape=(out, out),
        in_specs=[SMEM, VMEM, VMEM],
        out_specs=(VMEM, VMEM),
        scratch_shapes=[pltpu.VMEM((BLK, TILES, SUB, LANES), jnp.float32)],
        compiler_params=PARAMS,
        name="subtract",
    )(words, arrived, start)


def root_rows(swap, inverse_ref, r_high, r_low, out_ref):
    me = lax.axis_index("col")
    chips, height = out_ref.shape[:2]
    for distance in range(chips):
        base = ((me // CORES + distance) % chips * CORES + (me + swap) % CORES) * height
        strip = inverse_ref[pl.ds(pl.multiple_of(base, height), height)]
        out_ref[distance] = product(*split(strip), r_high[...], r_low[...])


def root_other_kernel(side, inverse_ref, *refs):
    pieces, (other_ref, high_ref, low_ref, gathered_ref) = refs[: 2 * side], refs[2 * side :]
    me = lax.axis_index("row")
    for i in range(side):
        for j in range(side):
            source = (me // side - i + side) % side * side + (me % side - j + side) % side
            gathered_ref[source, :, 0] = pieces[i][j]
            gathered_ref[source, :, 1] = pieces[side + j][i]
    join_slices(gathered_ref, high_ref, low_ref)
    root_rows(1, inverse_ref, high_ref, low_ref, other_ref)


def root_mine_kernel(high_ref, low_ref, inverse_ref, mine_ref):
    root_rows(0, inverse_ref, high_ref, low_ref, mine_ref)


def root(pieces, root_inverse, rows, chips):
    height, depth = root_inverse.shape
    out = f32(chips, height // (CORES * chips), NRHS)
    half = jax.ShapeDtypeStruct((depth, NRHS), jnp.bfloat16)
    cost = pl.CostEstimate(flops=3 * height * depth * NRHS, transcendentals=0, bytes_accessed=2 * height * depth)
    other, high, low = pl.pallas_call(
        functools.partial(root_other_kernel, len(pieces) // 2),
        out_shape=(out, half, half),
        in_specs=[VMEM] * (1 + len(pieces)),
        out_specs=(VMEM,) * 3,
        scratch_shapes=[pltpu.VMEM((rows, depth // BLK, TILES, SUB, LANES), jnp.float32)],
        compiler_params=PARAMS,
        cost_estimate=cost,
        name="root_other",
    )(root_inverse, *pieces)
    mine = pl.pallas_call(
        root_mine_kernel,
        out_shape=out,
        in_specs=[VMEM] * 3,
        out_specs=VMEM,
        compiler_params=PARAMS,
        cost_estimate=cost,
        name="root_mine",
    )(high, low, root_inverse)
    return mine, other


def reduce_cols(mine, other, cols):
    chips = cols // CORES
    sibling = lax.ppermute(other, "col", [(c, c ^ 1) for c in range(cols)])
    total = mine[0] + sibling[0]
    parts = [
        lax.ppermute(
            mine[distance] + sibling[distance], "col", [(c, (c + CORES * distance) % cols) for c in range(cols)]
        )
        for distance in range(1, chips)
    ]
    for part in parts:
        total = total + part
    return total


def gather_rows(piece, rows, side):
    def along_y(x):
        return [x] + [
            lax.ppermute(x, "row", [(i, i // side * side + (i + k) % side) for i in range(rows)])
            for k in range(1, side)
        ]

    def along_z(x):
        return [x] + [lax.ppermute(x, "row", [(i, (i + side * k) % rows) for i in range(rows)]) for k in range(1, side)]

    first, second = lax.optimization_barrier((along_y(piece[:, 0]), along_z(piece[:, 1])))
    first, second = lax.optimization_barrier((jnp.stack(first), jnp.stack(second)))
    return along_z(first) + along_y(second)


def shards(rhs, block_target, pivot_inverse, update_factor, root_inverse, update_map):
    rows = lax.axis_size("row")
    cols = lax.axis_size("col")
    chips = cols // CORES
    half = update_map.shape[0]
    arrived = exchange(pack(rhs, block_target, update_map, rows), "row")
    send, direct, words = route(arrived, rows, half, chips)
    pivot = exchange(send.reshape(rows, half, TILES, SUB, LANES), "row")
    solved, update = front(pivot, pivot_inverse, update_factor)
    returned = exchange(update, "row")
    piece = reduce_cols(*subtract(words, returned, direct, chips), cols)
    pieces = gather_rows(piece, rows, math.isqrt(rows))
    root_solution = reduce_cols(*root(pieces, root_inverse, rows, chips), cols)
    return (solved, root_solution)


def solution(mesh):
    return jax.shard_map(
        shards,
        mesh=mesh,
        in_specs=(
            P(("row", "col"), None),
            P(("row", "col")),
            P(("row", "col"), None),
            P(("row", "col"), None),
            P("row", "col"),
            P(("row", "col")),
        ),
        out_specs=(P(("row", "col"), None), P(("row", "col"), None)),
        check_vma=False,
    )
```

```python
import functools
import math

import jax
import jax.numpy as jnp
from jax import lax
from jax.experimental import pallas as pl
from jax.experimental.pallas import tpu as pltpu
from jax.sharding import PartitionSpec as P

BLK = 128
NRHS = 256
RB_DEV = 16
SUB = 8
LANES = 128
TILES = NRHS // LANES
CORES = 2
VMEM_LIMIT = 8 << 20
TILE = 256
VMEM = pl.BlockSpec(memory_space=pltpu.VMEM)
SMEM = pl.BlockSpec(memory_space=pltpu.SMEM)
ANY = pl.BlockSpec(memory_space=pl.ANY)
PARAMS = pltpu.CompilerParams(vmem_limit_bytes=VMEM_LIMIT)


def f32(*shape):
    return jax.ShapeDtypeStruct(shape, jnp.float32)


def far(x):
    return pltpu.with_memory_space_constraint(x, pltpu.HBM)


def split(x):
    high = x.astype(jnp.bfloat16)
    low = (x - high.astype(jnp.float32)).astype(jnp.bfloat16)
    return high, low


def product(a_high, a_low, b_high, b_low):
    out = jnp.dot(a_high, b_high, preferred_element_type=jnp.float32)
    out += jnp.dot(a_high, b_low, preferred_element_type=jnp.float32)
    out += jnp.dot(a_low, b_high, preferred_element_type=jnp.float32)
    return out


def exchange(x, axis):
    return lax.all_to_all(x, axis, split_axis=0, concat_axis=0, tiled=True)


def pack_kernel(rows, half, target_ref, map_ref, rhs_ref, out_ref, targets, roots, sems, table_sems):
    tables = [
        pltpu.make_async_copy(target_ref, targets, table_sems.at[0]),
        pltpu.make_async_copy(map_ref, roots, table_sems.at[1]),
    ]
    copies = [
        pltpu.make_async_copy(
            rhs_ref.at[block, :, :, pl.ds(lane * LANES, LANES)],
            out_ref.at[:, block * TILES + lane],
            sems.at[block * TILES + lane],
        )
        for block in range(RB_DEV)
        for lane in range(TILES)
    ]
    for copy in tables + copies:
        copy.start()
    for copy in tables:
        copy.wait()
    lane = lax.broadcasted_iota(jnp.int32, (SUB, LANES), 1)
    words = jnp.zeros((SUB, LANES), jnp.int32)
    for i in range(RB_DEV):
        words = jnp.where(lane == i, targets[i], words)
    for i in range(half):
        words = jnp.where(lane == RB_DEV + i, roots[i], words)
    words = words.astype(jnp.float32)
    for peer in range(rows):
        out_ref[peer, RB_DEV * TILES] = words
    for copy in copies:
        copy.wait()


def pack(rhs, block_target, update_map, rows):
    half = update_map.shape[0]
    return pl.pallas_call(
        functools.partial(pack_kernel, rows, half),
        out_shape=f32(rows, RB_DEV * TILES + 1, SUB, LANES),
        in_specs=[ANY] * 3,
        out_specs=VMEM,
        scratch_shapes=[
            pltpu.SMEM((RB_DEV,), jnp.int32),
            pltpu.SMEM((half,), jnp.int32),
            pltpu.SemaphoreType.DMA((RB_DEV * TILES,)),
            pltpu.SemaphoreType.DMA((2,)),
        ],
        compiler_params=PARAMS,
        name="pack",
    )(far(block_target), far(update_map), far(rhs.reshape(RB_DEV, rows, SUB, NRHS)))


def relative(root, per_col, chips):
    me = lax.axis_index("col")
    col = root // per_col
    distance = (col // CORES - me // CORES + chips) % chips
    other = (col + me) % CORES
    return (other * chips + distance) * per_col + root % per_col


def route_kernel(rows, half, chips, arrived_ref, send_ref, acc_ref, words, table, sem):
    slots = rows * half
    received = arrived_ref[:, RB_DEV * TILES, 0].astype(jnp.int32)
    lane = lax.broadcasted_iota(jnp.int32, received.shape, 1)
    owner = received // RB_DEV
    slot = received % RB_DEV
    entry = owner * half + slot + jnp.where(slot < half, 0, slots - half)
    words[...] = jnp.where(lane < RB_DEV, entry, slots + relative(received, BLK // (CORES * chips), chips))
    copy = pltpu.make_async_copy(words, table, sem)
    copy.start()
    acc_ref[...] = jnp.zeros_like(acc_ref)
    copy.wait()

    def place(source, carry):
        for block in range(RB_DEV):
            where = table[source, block]
            update = where >= slots
            index = lax.bitwise_and(where, slots - 1)
            root = table[lax.shift_right_logical(index, half.bit_length() - 1), RB_DEV + lax.bitwise_and(index, half - 1)]
            position = jnp.where(update, root, index)
            acc_ref[position] += arrived_ref[source, pl.ds(block * TILES, TILES)]
        return carry

    lax.fori_loop(0, rows, place, 0)
    send_ref[...] = acc_ref[pl.ds(0, slots)]


def route(arrived, rows, half, chips):
    slots = rows * half
    return pl.pallas_call(
        functools.partial(route_kernel, rows, half, chips),
        out_shape=(
            f32(slots, TILES, SUB, LANES),
            f32(slots + BLK, TILES, SUB, LANES),
            jax.ShapeDtypeStruct((rows, LANES), jnp.int32),
        ),
        in_specs=[VMEM],
        out_specs=(VMEM, VMEM, VMEM),
        scratch_shapes=[
            pltpu.SMEM((rows, LANES), jnp.int32),
            pltpu.SemaphoreType.DMA,
        ],
        compiler_params=PARAMS,
        name="route",
    )(arrived)


def split_into(value, high_ref, low_ref, start, lane=0):
    high, low = split(value)
    here = (pl.ds(start, value.shape[0]), pl.ds(lane * LANES, value.shape[1]))
    high_ref[here] = high
    low_ref[here] = low


def join_slices(slices_ref, high_ref, low_ref):
    for block in range(slices_ref.shape[1]):
        for lane in range(TILES):
            split_into(slices_ref[:, block, lane].reshape(BLK, LANES), high_ref, low_ref, block * BLK, lane)


def front_kernel(arrived_ref, pivot_ref, factor_ref, solved_ref, update_ref, p_high, p_low, s_high, s_low):
    rows, blocks = arrived_ref.shape[:2]
    order = blocks * BLK
    join_slices(arrived_ref, p_high, p_low)
    for start in range(0, order, TILE):
        here, depth = pl.ds(start, TILE), pl.ds(0, start + TILE)
        value = product(*split(pivot_ref[here, depth]), p_high[depth], p_low[depth])
        solved_ref[here] = value
        split_into(value, s_high, s_low, start)
    for start in range(0, order, TILE):
        value = product(*split(factor_ref[pl.ds(start, TILE)]), s_high[...], s_low[...])
        for block in range(TILE // BLK):
            for lane in range(TILES):
                part = value[block * BLK : (block + 1) * BLK, lane * LANES : (lane + 1) * LANES]
                update_ref[:, start // BLK + block, lane] = part.reshape(rows, SUB, LANES)


def front(arrived, pivot_inverse, update_factor):
    rows, half = arrived.shape[:2]
    order = half * BLK
    return pl.pallas_call(
        front_kernel,
        out_shape=(f32(order, NRHS), f32(rows, half, TILES, SUB, LANES)),
        in_specs=[VMEM] * 3,
        out_specs=(VMEM, VMEM),
        scratch_shapes=[pltpu.VMEM((order, NRHS), jnp.bfloat16)] * 4,
        compiler_params=PARAMS,
        name="front",
    )(arrived, pivot_inverse, update_factor)


def subtract_kernel(rows, half, words_ref, arrived_ref, start_ref, mine_ref, other_ref, acc):
    slots = rows * half
    acc[...] = start_ref[pl.ds(slots, BLK)]

    def add(owner, carry):
        for block in range(half):
            acc[words_ref[owner, RB_DEV + block] - slots] -= arrived_ref[owner, block]
        return carry

    lax.fori_loop(0, rows, add, 0)
    part = mine_ref.shape[:1] + mine_ref.shape[2:]
    for lane in range(TILES):
        mine_ref[:, lane] = acc[pl.ds(0, BLK // CORES), lane].reshape(part)
        other_ref[:, lane] = acc[pl.ds(BLK // CORES, BLK // CORES), lane].reshape(part)


def subtract(words, arrived, start, chips):
    rows, half = arrived.shape[:2]
    out = f32(chips, TILES, BLK // (CORES * chips), SUB, LANES)
    return pl.pallas_call(
        functools.partial(subtract_kernel, rows, half),
        out_shape=(out, out),
        in_specs=[SMEM, VMEM, VMEM],
        out_specs=(VMEM, VMEM),
        scratch_shapes=[pltpu.VMEM((BLK, TILES, SUB, LANES), jnp.float32)],
        compiler_params=PARAMS,
        name="subtract",
    )(words, arrived, start)


def root_rows(swap, inverse_ref, r_high, r_low, out_ref):
    me = lax.axis_index("col")
    chips, height = out_ref.shape[:2]
    for distance in range(chips):
        base = ((me // CORES + distance) % chips * CORES + (me + swap) % CORES) * height
        strip = inverse_ref[pl.ds(pl.multiple_of(base, height), height)]
        out_ref[distance] = product(*split(strip), r_high[...], r_low[...])


def root_other_kernel(side, inverse_ref, *refs):
    pieces, (other_ref, high_ref, low_ref, gathered_ref) = refs[: 2 * side], refs[2 * side :]
    me = lax.axis_index("row")
    for i, z in enumerate(shifts(side)):
        for j, y in enumerate(shifts(side)):
            source = (me // side - z + side) % side * side + (me % side - y + side) % side
            gathered_ref[source, :, 0] = pieces[i][j]
            gathered_ref[source, :, 1] = pieces[side + j][i]
    join_slices(gathered_ref, high_ref, low_ref)
    root_rows(1, inverse_ref, high_ref, low_ref, other_ref)


def root_mine_kernel(high_ref, low_ref, inverse_ref, mine_ref):
    root_rows(0, inverse_ref, high_ref, low_ref, mine_ref)


def root(pieces, root_inverse, rows, chips):
    height, depth = root_inverse.shape
    out = f32(chips, height // (CORES * chips), NRHS)
    half = jax.ShapeDtypeStruct((depth, NRHS), jnp.bfloat16)
    cost = pl.CostEstimate(flops=3 * height * depth * NRHS, transcendentals=0, bytes_accessed=2 * height * depth)
    other, high, low = pl.pallas_call(
        functools.partial(root_other_kernel, len(pieces) // 2),
        out_shape=(out, half, half),
        in_specs=[VMEM] * (1 + len(pieces)),
        out_specs=(VMEM,) * 3,
        scratch_shapes=[pltpu.VMEM((rows, depth // BLK, TILES, SUB, LANES), jnp.float32)],
        compiler_params=PARAMS,
        cost_estimate=cost,
        name="root_other",
    )(root_inverse, *pieces)
    mine = pl.pallas_call(
        root_mine_kernel,
        out_shape=out,
        in_specs=[VMEM] * 3,
        out_specs=VMEM,
        compiler_params=PARAMS,
        cost_estimate=cost,
        name="root_mine",
    )(high, low, root_inverse)
    return mine, other


def reduce_cols(mine, other, cols):
    chips = cols // CORES
    sibling = lax.ppermute(other, "col", [(c, c ^ 1) for c in range(cols)])
    total = mine[0] + sibling[0]
    parts = [
        lax.ppermute(
            mine[distance] + sibling[distance], "col", [(c, (c + CORES * distance) % cols) for c in range(cols)]
        )
        for distance in range(1, chips)
    ]
    for part in parts:
        total = total + part
    return total


def shifts(side):
    return sorted(range(side), key=lambda k: (k > 0, k != side // 2, k))


def gather_rows(piece, rows, side):
    def along_y(x):
        pairs = lambda k: [(i, i // side * side + (i + k) % side) for i in range(rows)]
        return [x] + [lax.ppermute(x, "row", pairs(k)) for k in shifts(side)[1:]]

    def along_z(x):
        pairs = lambda k: [(i, (i + side * k) % rows) for i in range(rows)]
        return [x] + [lax.ppermute(x, "row", pairs(k)) for k in shifts(side)[1:]]

    first, second = lax.optimization_barrier((along_y(piece[0]), along_z(piece[1])))
    first, second = lax.optimization_barrier((jnp.stack(first), jnp.stack(second)))
    return along_z(first) + along_y(second)


def shards(rhs, block_target, pivot_inverse, update_factor, root_inverse, update_map):
    rows = lax.axis_size("row")
    cols = lax.axis_size("col")
    chips = cols // CORES
    half = update_map.shape[0]
    arrived = exchange(pack(rhs, block_target, update_map, rows), "row")
    send, direct, words = route(arrived, rows, half, chips)
    pivot = exchange(send.reshape(rows, half, TILES, SUB, LANES), "row")
    solved, update = front(pivot, pivot_inverse, update_factor)
    returned = exchange(update, "row")
    piece = reduce_cols(*subtract(words, returned, direct, chips), cols)
    pieces = gather_rows(piece, rows, math.isqrt(rows))
    root_solution = reduce_cols(*root(pieces, root_inverse, rows, chips), cols)
    return (solved, root_solution)


def solution(mesh):
    return jax.shard_map(
        shards,
        mesh=mesh,
        in_specs=(
            P(("row", "col"), None),
            P(("row", "col")),
            P(("row", "col"), None),
            P(("row", "col"), None),
            P("row", "col"),
            P(("row", "col")),
        ),
        out_specs=(P(("row", "col"), None), P(("row", "col"), None)),
        check_vma=False,
    )
```

```python
import functools
import math

import jax
import jax.numpy as jnp
from jax import lax
from jax.experimental import pallas as pl
from jax.experimental.pallas import tpu as pltpu
from jax.sharding import PartitionSpec as P

BLK = 128
NRHS = 256
RB_DEV = 16
SUB = 8
LANES = 128
TILES = NRHS // LANES
CORES = 2
VMEM_LIMIT = 8 << 20
TILE = 256
VMEM = pl.BlockSpec(memory_space=pltpu.VMEM)
SMEM = pl.BlockSpec(memory_space=pltpu.SMEM)
ANY = pl.BlockSpec(memory_space=pl.ANY)
PARAMS = pltpu.CompilerParams(vmem_limit_bytes=VMEM_LIMIT)


def f32(*shape):
    return jax.ShapeDtypeStruct(shape, jnp.float32)


def far(x):
    return pltpu.with_memory_space_constraint(x, pltpu.HBM)


def split(x):
    high = x.astype(jnp.bfloat16)
    low = (x - high.astype(jnp.float32)).astype(jnp.bfloat16)
    return high, low


def product(a_high, a_low, b_high, b_low):
    out = jnp.dot(a_high, b_high, preferred_element_type=jnp.float32)
    out += jnp.dot(a_high, b_low, preferred_element_type=jnp.float32)
    out += jnp.dot(a_low, b_high, preferred_element_type=jnp.float32)
    return out


def exchange(x, axis):
    return lax.all_to_all(x, axis, split_axis=0, concat_axis=0, tiled=True)


def pack_kernel(rows, half, target_ref, map_ref, rhs_ref, out_ref, targets, roots, sems, table_sems):
    tables = [
        pltpu.make_async_copy(target_ref, targets, table_sems.at[0]),
        pltpu.make_async_copy(map_ref, roots, table_sems.at[1]),
    ]
    copies = [
        pltpu.make_async_copy(
            rhs_ref.at[block, :, :, pl.ds(lane * LANES, LANES)],
            out_ref.at[:, block * TILES + lane],
            sems.at[block * TILES + lane],
        )
        for block in range(RB_DEV)
        for lane in range(TILES)
    ]
    for copy in tables + copies:
        copy.start()
    for copy in tables:
        copy.wait()
    lane = lax.broadcasted_iota(jnp.int32, (SUB, LANES), 1)
    words = jnp.zeros((SUB, LANES), jnp.int32)
    for i in range(RB_DEV):
        words = jnp.where(lane == i, targets[i], words)
    for i in range(half):
        words = jnp.where(lane == RB_DEV + i, roots[i], words)
    words = words.astype(jnp.float32)
    for peer in range(rows):
        out_ref[peer, RB_DEV * TILES] = words
    for copy in copies:
        copy.wait()


def pack(rhs, block_target, update_map, rows):
    half = update_map.shape[0]
    return pl.pallas_call(
        functools.partial(pack_kernel, rows, half),
        out_shape=f32(rows, RB_DEV * TILES + 1, SUB, LANES),
        in_specs=[ANY] * 3,
        out_specs=VMEM,
        scratch_shapes=[
            pltpu.SMEM((RB_DEV,), jnp.int32),
            pltpu.SMEM((half,), jnp.int32),
            pltpu.SemaphoreType.DMA((RB_DEV * TILES,)),
            pltpu.SemaphoreType.DMA((2,)),
        ],
        compiler_params=PARAMS,
        name="pack",
    )(far(block_target), far(update_map), far(rhs.reshape(RB_DEV, rows, SUB, NRHS)))


def relative(root, per_col, chips):
    me = lax.axis_index("col")
    col = root // per_col
    distance = (col // CORES - me // CORES + chips) % chips
    other = (col + me) % CORES
    return (other * chips + distance) * per_col + root % per_col


def route_kernel(rows, half, chips, arrived_ref, send_ref, acc_ref, words, table, sem):
    slots = rows * half
    received = arrived_ref[:, RB_DEV * TILES, 0].astype(jnp.int32)
    lane = lax.broadcasted_iota(jnp.int32, received.shape, 1)
    owner = received // RB_DEV
    slot = received % RB_DEV
    entry = owner * half + slot + jnp.where(slot < half, 0, slots - half)
    words[...] = jnp.where(lane < RB_DEV, entry, slots + relative(received, BLK // (CORES * chips), chips))
    copy = pltpu.make_async_copy(words, table, sem)
    copy.start()
    acc_ref[...] = jnp.zeros_like(acc_ref)
    copy.wait()

    def place(source, carry):
        for block in range(RB_DEV):
            where = table[source, block]
            update = where >= slots
            index = lax.bitwise_and(where, slots - 1)
            root = table[lax.shift_right_logical(index, half.bit_length() - 1), RB_DEV + lax.bitwise_and(index, half - 1)]
            position = jnp.where(update, root, index)
            acc_ref[position] += arrived_ref[source, pl.ds(block * TILES, TILES)]
        return carry

    lax.fori_loop(0, rows, place, 0)
    send_ref[...] = acc_ref[pl.ds(0, slots)]


def route(arrived, rows, half, chips):
    slots = rows * half
    return pl.pallas_call(
        functools.partial(route_kernel, rows, half, chips),
        out_shape=(
            f32(slots, TILES, SUB, LANES),
            f32(slots + BLK, TILES, SUB, LANES),
            jax.ShapeDtypeStruct((rows, LANES), jnp.int32),
        ),
        in_specs=[VMEM],
        out_specs=(VMEM, VMEM, VMEM),
        scratch_shapes=[
            pltpu.SMEM((rows, LANES), jnp.int32),
            pltpu.SemaphoreType.DMA,
        ],
        compiler_params=PARAMS,
        name="route",
    )(arrived)


def split_into(value, high_ref, low_ref, start, lane=0):
    high, low = split(value)
    here = (pl.ds(start, value.shape[0]), pl.ds(lane * LANES, value.shape[1]))
    high_ref[here] = high
    low_ref[here] = low


def join_slices(slices_ref, high_ref, low_ref):
    for block in range(slices_ref.shape[1]):
        for lane in range(TILES):
            split_into(slices_ref[:, block, lane].reshape(BLK, LANES), high_ref, low_ref, block * BLK, lane)


def front_kernel(arrived_ref, pivot_ref, factor_ref, solved_ref, update_ref, p_high, p_low, s_high, s_low):
    rows, blocks = arrived_ref.shape[:2]
    order = blocks * BLK
    join_slices(arrived_ref, p_high, p_low)
    for start in range(0, order, TILE):
        here, depth = pl.ds(start, TILE), pl.ds(0, start + TILE)
        value = product(*split(pivot_ref[here, depth]), p_high[depth], p_low[depth])
        solved_ref[here] = value
        split_into(value, s_high, s_low, start)
    for start in range(0, order, TILE):
        value = product(*split(factor_ref[pl.ds(start, TILE)]), s_high[...], s_low[...])
        for block in range(TILE // BLK):
            for lane in range(TILES):
                part = value[block * BLK : (block + 1) * BLK, lane * LANES : (lane + 1) * LANES]
                update_ref[:, start // BLK + block, lane] = part.reshape(rows, SUB, LANES)


def front(arrived, pivot_inverse, update_factor):
    rows, half = arrived.shape[:2]
    order = half * BLK
    return pl.pallas_call(
        front_kernel,
        out_shape=(f32(order, NRHS), f32(rows, half, TILES, SUB, LANES)),
        in_specs=[VMEM] * 3,
        out_specs=(VMEM, VMEM),
        scratch_shapes=[pltpu.VMEM((order, NRHS), jnp.bfloat16)] * 4,
        compiler_params=PARAMS,
        name="front",
    )(arrived, pivot_inverse, update_factor)


def subtract_kernel(rows, half, words_ref, arrived_ref, start_ref, mine_ref, other_ref, acc, table, sem):
    slots = rows * half
    copy = pltpu.make_async_copy(words_ref, table, sem)
    copy.start()
    acc[...] = start_ref[pl.ds(slots, BLK)]
    copy.wait()

    def add(owner, carry):
        for block in range(half):
            acc[table[owner, RB_DEV + block] - slots] -= arrived_ref[owner, block]
        return carry

    lax.fori_loop(0, rows, add, 0)
    part = mine_ref.shape[:1] + mine_ref.shape[2:]
    for lane in range(TILES):
        mine_ref[:, lane] = acc[pl.ds(0, BLK // CORES), lane].reshape(part)
        other_ref[:, lane] = acc[pl.ds(BLK // CORES, BLK // CORES), lane].reshape(part)


def subtract(words, arrived, start, chips):
    rows, half = arrived.shape[:2]
    out = f32(chips, TILES, BLK // (CORES * chips), SUB, LANES)
    return pl.pallas_call(
        functools.partial(subtract_kernel, rows, half),
        out_shape=(out, out),
        in_specs=[VMEM] * 3,
        out_specs=(VMEM, VMEM),
        scratch_shapes=[
            pltpu.VMEM((BLK, TILES, SUB, LANES), jnp.float32),
            pltpu.SMEM((rows, LANES), jnp.int32),
            pltpu.SemaphoreType.DMA,
        ],
        compiler_params=PARAMS,
        name="subtract",
    )(words, arrived, start)


def root_rows(swap, inverse_ref, r_high, r_low, out_ref):
    me = lax.axis_index("col")
    chips, height = out_ref.shape[:2]
    for distance in range(chips):
        base = ((me // CORES + distance) % chips * CORES + (me + swap) % CORES) * height
        strip = inverse_ref[pl.ds(pl.multiple_of(base, height), height)]
        out_ref[distance] = product(*split(strip), r_high[...], r_low[...])


def root_other_kernel(side, inverse_ref, *refs):
    pieces, (other_ref, high_ref, low_ref, gathered_ref) = refs[: 2 * side], refs[2 * side :]
    me = lax.axis_index("row")
    for i in range(side):
        for j in range(side):
            source = (me // side - i + side) % side * side + (me % side - j + side) % side
            gathered_ref[source, :, 0] = pieces[i][j]
            gathered_ref[source, :, 1] = pieces[side + j][i]
    join_slices(gathered_ref, high_ref, low_ref)
    root_rows(1, inverse_ref, high_ref, low_ref, other_ref)


def root_mine_kernel(high_ref, low_ref, inverse_ref, mine_ref):
    root_rows(0, inverse_ref, high_ref, low_ref, mine_ref)


def root(pieces, root_inverse, rows, chips):
    height, depth = root_inverse.shape
    out = f32(chips, height // (CORES * chips), NRHS)
    half = jax.ShapeDtypeStruct((depth, NRHS), jnp.bfloat16)
    cost = pl.CostEstimate(flops=3 * height * depth * NRHS, transcendentals=0, bytes_accessed=2 * height * depth)
    other, high, low = pl.pallas_call(
        functools.partial(root_other_kernel, len(pieces) // 2),
        out_shape=(out, half, half),
        in_specs=[VMEM] * (1 + len(pieces)),
        out_specs=(VMEM,) * 3,
        scratch_shapes=[pltpu.VMEM((rows, depth // BLK, TILES, SUB, LANES), jnp.float32)],
        compiler_params=PARAMS,
        cost_estimate=cost,
        name="root_other",
    )(root_inverse, *pieces)
    mine = pl.pallas_call(
        root_mine_kernel,
        out_shape=out,
        in_specs=[VMEM] * 3,
        out_specs=VMEM,
        compiler_params=PARAMS,
        cost_estimate=cost,
        name="root_mine",
    )(high, low, root_inverse)
    return mine, other


def reduce_cols(mine, other, cols):
    chips = cols // CORES
    sibling = lax.ppermute(other, "col", [(c, c ^ 1) for c in range(cols)])
    total = mine[0] + sibling[0]
    parts = [
        lax.ppermute(
            mine[distance] + sibling[distance], "col", [(c, (c + CORES * distance) % cols) for c in range(cols)]
        )
        for distance in range(1, chips)
    ]
    for part in parts:
        total = total + part
    return total


def gather_rows(piece, rows, side):
    def along_y(x):
        return [x] + [
            lax.ppermute(x, "row", [(i, i // side * side + (i + k) % side) for i in range(rows)])
            for k in range(1, side)
        ]

    def along_z(x):
        return [x] + [lax.ppermute(x, "row", [(i, (i + side * k) % rows) for i in range(rows)]) for k in range(1, side)]

    first, second = lax.optimization_barrier((along_y(piece[0]), along_z(piece[1])))
    first, second = lax.optimization_barrier((jnp.stack(first), jnp.stack(second)))
    return along_z(first) + along_y(second)


def shards(rhs, block_target, pivot_inverse, update_factor, root_inverse, update_map):
    rows = lax.axis_size("row")
    cols = lax.axis_size("col")
    chips = cols // CORES
    half = update_map.shape[0]
    arrived = exchange(pack(rhs, block_target, update_map, rows), "row")
    send, direct, words = route(arrived, rows, half, chips)
    pivot = exchange(send.reshape(rows, half, TILES, SUB, LANES), "row")
    solved, update = front(pivot, pivot_inverse, update_factor)
    returned = exchange(update, "row")
    piece = reduce_cols(*subtract(words, returned, direct, chips), cols)
    pieces = gather_rows(piece, rows, math.isqrt(rows))
    root_solution = reduce_cols(*root(pieces, root_inverse, rows, chips), cols)
    return (solved, root_solution)


def solution(mesh):
    return jax.shard_map(
        shards,
        mesh=mesh,
        in_specs=(
            P(("row", "col"), None),
            P(("row", "col")),
            P(("row", "col"), None),
            P(("row", "col"), None),
            P("row", "col"),
            P(("row", "col")),
        ),
        out_specs=(P(("row", "col"), None), P(("row", "col"), None)),
        check_vma=False,
    )
```

```python
import functools
import math

import jax
import jax.numpy as jnp
from jax import lax
from jax.experimental import pallas as pl
from jax.experimental.pallas import tpu as pltpu
from jax.sharding import PartitionSpec as P

BLK = 128
NRHS = 256
RB_DEV = 16
SUB = 8
LANES = 128
TILES = NRHS // LANES
CORES = 2
VMEM_LIMIT = 8 << 20
TILE = 128
VMEM = pl.BlockSpec(memory_space=pltpu.VMEM)
SMEM = pl.BlockSpec(memory_space=pltpu.SMEM)
ANY = pl.BlockSpec(memory_space=pl.ANY)
PARAMS = pltpu.CompilerParams(vmem_limit_bytes=VMEM_LIMIT)


def f32(*shape):
    return jax.ShapeDtypeStruct(shape, jnp.float32)


def far(x):
    return pltpu.with_memory_space_constraint(x, pltpu.HBM)


def split(x):
    high = x.astype(jnp.bfloat16)
    low = (x - high.astype(jnp.float32)).astype(jnp.bfloat16)
    return high, low


def product(a_high, a_low, b_high, b_low):
    out = jnp.dot(a_high, b_high, preferred_element_type=jnp.float32)
    out += jnp.dot(a_high, b_low, preferred_element_type=jnp.float32)
    out += jnp.dot(a_low, b_high, preferred_element_type=jnp.float32)
    return out


def exchange(x, axis):
    return lax.all_to_all(x, axis, split_axis=0, concat_axis=0, tiled=True)


def pack_kernel(rows, half, target_ref, map_ref, rhs_ref, out_ref, targets, roots, sems, table_sems):
    tables = [
        pltpu.make_async_copy(target_ref, targets, table_sems.at[0]),
        pltpu.make_async_copy(map_ref, roots, table_sems.at[1]),
    ]
    copies = [
        pltpu.make_async_copy(
            rhs_ref.at[block, :, :, pl.ds(lane * LANES, LANES)],
            out_ref.at[:, block * TILES + lane],
            sems.at[block * TILES + lane],
        )
        for block in range(RB_DEV)
        for lane in range(TILES)
    ]
    for copy in tables + copies:
        copy.start()
    for copy in tables:
        copy.wait()
    lane = lax.broadcasted_iota(jnp.int32, (SUB, LANES), 1)
    words = jnp.zeros((SUB, LANES), jnp.int32)
    for i in range(RB_DEV):
        words = jnp.where(lane == i, targets[i], words)
    for i in range(half):
        words = jnp.where(lane == RB_DEV + i, roots[i], words)
    words = words.astype(jnp.float32)
    for peer in range(rows):
        out_ref[peer, RB_DEV * TILES] = words
    for copy in copies:
        copy.wait()


def pack(rhs, block_target, update_map, rows):
    half = update_map.shape[0]
    return pl.pallas_call(
        functools.partial(pack_kernel, rows, half),
        out_shape=f32(rows, RB_DEV * TILES + 1, SUB, LANES),
        in_specs=[ANY] * 3,
        out_specs=VMEM,
        scratch_shapes=[
            pltpu.SMEM((RB_DEV,), jnp.int32),
            pltpu.SMEM((half,), jnp.int32),
            pltpu.SemaphoreType.DMA((RB_DEV * TILES,)),
            pltpu.SemaphoreType.DMA((2,)),
        ],
        compiler_params=PARAMS,
        name="pack",
    )(far(block_target), far(update_map), far(rhs.reshape(RB_DEV, rows, SUB, NRHS)))


def relative(root, per_col, chips):
    me = lax.axis_index("col")
    col = root // per_col
    distance = (col // CORES - me // CORES + chips) % chips
    other = (col + me) % CORES
    return (other * chips + distance) * per_col + root % per_col


def route_kernel(rows, half, chips, arrived_ref, send_ref, acc_ref, words, table, sem):
    slots = rows * half
    received = arrived_ref[:, RB_DEV * TILES, 0].astype(jnp.int32)
    lane = lax.broadcasted_iota(jnp.int32, received.shape, 1)
    owner = received // RB_DEV
    slot = received % RB_DEV
    entry = owner * half + slot + jnp.where(slot < half, 0, slots - half)
    words[...] = jnp.where(lane < RB_DEV, entry, slots + relative(received, BLK // (CORES * chips), chips))
    copy = pltpu.make_async_copy(words, table, sem)
    copy.start()
    acc_ref[...] = jnp.zeros_like(acc_ref)
    copy.wait()

    def place(source, carry):
        for block in range(RB_DEV):
            where = table[source, block]
            update = where >= slots
            index = lax.bitwise_and(where, slots - 1)
            root = table[lax.shift_right_logical(index, half.bit_length() - 1), RB_DEV + lax.bitwise_and(index, half - 1)]
            position = jnp.where(update, root, index)
            acc_ref[position] += arrived_ref[source, pl.ds(block * TILES, TILES)]
        return carry

    lax.fori_loop(0, rows, place, 0)
    send_ref[...] = acc_ref[pl.ds(0, slots)]


def route(arrived, rows, half, chips):
    slots = rows * half
    return pl.pallas_call(
        functools.partial(route_kernel, rows, half, chips),
        out_shape=(
            f32(slots, TILES, SUB, LANES),
            f32(slots + BLK, TILES, SUB, LANES),
            jax.ShapeDtypeStruct((rows, LANES), jnp.int32),
        ),
        in_specs=[VMEM],
        out_specs=(VMEM, VMEM, VMEM),
        scratch_shapes=[
            pltpu.SMEM((rows, LANES), jnp.int32),
            pltpu.SemaphoreType.DMA,
        ],
        compiler_params=PARAMS,
        name="route",
    )(arrived)


def split_into(value, high_ref, low_ref, start, lane=0):
    high, low = split(value)
    here = (pl.ds(start, value.shape[0]), pl.ds(lane * LANES, value.shape[1]))
    high_ref[here] = high
    low_ref[here] = low


def join_slices(slices_ref, high_ref, low_ref):
    for block in range(slices_ref.shape[1]):
        for lane in range(TILES):
            split_into(slices_ref[:, block, lane].reshape(BLK, LANES), high_ref, low_ref, block * BLK, lane)


def front_kernel(arrived_ref, pivot_ref, factor_ref, solved_ref, update_ref, p_high, p_low, s_high, s_low):
    rows, blocks = arrived_ref.shape[:2]
    order = blocks * BLK
    join_slices(arrived_ref, p_high, p_low)
    for start in range(0, order, TILE):
        here, depth = pl.ds(start, TILE), pl.ds(0, start + TILE)
        value = product(*split(pivot_ref[here, depth]), p_high[depth], p_low[depth])
        solved_ref[here] = value
        split_into(value, s_high, s_low, start)
    for start in range(0, order, TILE):
        value = product(*split(factor_ref[pl.ds(start, TILE)]), s_high[...], s_low[...])
        for block in range(TILE // BLK):
            for lane in range(TILES):
                part = value[block * BLK : (block + 1) * BLK, lane * LANES : (lane + 1) * LANES]
                update_ref[:, start // BLK + block, lane] = part.reshape(rows, SUB, LANES)


def front(arrived, pivot_inverse, update_factor):
    rows, half = arrived.shape[:2]
    order = half * BLK
    return pl.pallas_call(
        front_kernel,
        out_shape=(f32(order, NRHS), f32(rows, half, TILES, SUB, LANES)),
        in_specs=[VMEM] * 3,
        out_specs=(VMEM, VMEM),
        scratch_shapes=[pltpu.VMEM((order, NRHS), jnp.bfloat16)] * 4,
        compiler_params=PARAMS,
        name="front",
    )(arrived, pivot_inverse, update_factor)


def subtract_kernel(rows, half, words_ref, arrived_ref, start_ref, mine_ref, other_ref, acc, table, sem):
    slots = rows * half
    copy = pltpu.make_async_copy(words_ref, table, sem)
    copy.start()
    acc[...] = start_ref[pl.ds(slots, BLK)]
    copy.wait()

    def add(owner, carry):
        for block in range(half):
            acc[table[owner, RB_DEV + block] - slots] -= arrived_ref[owner, block]
        return carry

    lax.fori_loop(0, rows, add, 0)
    part = mine_ref.shape[:1] + mine_ref.shape[2:]
    for lane in range(TILES):
        mine_ref[:, lane] = acc[pl.ds(0, BLK // CORES), lane].reshape(part)
        other_ref[:, lane] = acc[pl.ds(BLK // CORES, BLK // CORES), lane].reshape(part)


def subtract(words, arrived, start, chips):
    rows, half = arrived.shape[:2]
    out = f32(chips, TILES, BLK // (CORES * chips), SUB, LANES)
    return pl.pallas_call(
        functools.partial(subtract_kernel, rows, half),
        out_shape=(out, out),
        in_specs=[VMEM] * 3,
        out_specs=(VMEM, VMEM),
        scratch_shapes=[
            pltpu.VMEM((BLK, TILES, SUB, LANES), jnp.float32),
            pltpu.SMEM((rows, LANES), jnp.int32),
            pltpu.SemaphoreType.DMA,
        ],
        compiler_params=PARAMS,
        name="subtract",
    )(words, arrived, start)


def root_rows(swap, inverse_ref, r_high, r_low, out_ref):
    me = lax.axis_index("col")
    chips, height = out_ref.shape[:2]
    for distance in range(chips):
        base = ((me // CORES + distance) % chips * CORES + (me + swap) % CORES) * height
        strip = inverse_ref[pl.ds(pl.multiple_of(base, height), height)]
        out_ref[distance] = product(*split(strip), r_high[...], r_low[...])


def root_other_kernel(side, inverse_ref, *refs):
    pieces, (other_ref, high_ref, low_ref, gathered_ref) = refs[: 2 * side], refs[2 * side :]
    me = lax.axis_index("row")
    for i in range(side):
        for j in range(side):
            source = (me // side - i + side) % side * side + (me % side - j + side) % side
            gathered_ref[source, :, 0] = pieces[i][j]
            gathered_ref[source, :, 1] = pieces[side + j][i]
    join_slices(gathered_ref, high_ref, low_ref)
    root_rows(1, inverse_ref, high_ref, low_ref, other_ref)


def root_mine_kernel(high_ref, low_ref, inverse_ref, mine_ref):
    root_rows(0, inverse_ref, high_ref, low_ref, mine_ref)


def root(pieces, root_inverse, rows, chips):
    height, depth = root_inverse.shape
    out = f32(chips, height // (CORES * chips), NRHS)
    half = jax.ShapeDtypeStruct((depth, NRHS), jnp.bfloat16)
    cost = pl.CostEstimate(flops=3 * height * depth * NRHS, transcendentals=0, bytes_accessed=2 * height * depth)
    other, high, low = pl.pallas_call(
        functools.partial(root_other_kernel, len(pieces) // 2),
        out_shape=(out, half, half),
        in_specs=[VMEM] * (1 + len(pieces)),
        out_specs=(VMEM,) * 3,
        scratch_shapes=[pltpu.VMEM((rows, depth // BLK, TILES, SUB, LANES), jnp.float32)],
        compiler_params=PARAMS,
        cost_estimate=cost,
        name="root_other",
    )(root_inverse, *pieces)
    mine = pl.pallas_call(
        root_mine_kernel,
        out_shape=out,
        in_specs=[VMEM] * 3,
        out_specs=VMEM,
        compiler_params=PARAMS,
        cost_estimate=cost,
        name="root_mine",
    )(high, low, root_inverse)
    return mine, other


def reduce_cols(mine, other, cols):
    chips = cols // CORES
    sibling = lax.ppermute(other, "col", [(c, c ^ 1) for c in range(cols)])
    total = mine[0] + sibling[0]
    parts = [
        lax.ppermute(
            mine[distance] + sibling[distance], "col", [(c, (c + CORES * distance) % cols) for c in range(cols)]
        )
        for distance in range(1, chips)
    ]
    for part in parts:
        total = total + part
    return total


def gather_rows(piece, rows, side):
    def along_y(x):
        return [x] + [
            lax.ppermute(x, "row", [(i, i // side * side + (i + k) % side) for i in range(rows)])
            for k in range(1, side)
        ]

    def along_z(x):
        return [x] + [lax.ppermute(x, "row", [(i, (i + side * k) % rows) for i in range(rows)]) for k in range(1, side)]

    first, second = lax.optimization_barrier((along_y(piece[0]), along_z(piece[1])))
    first, second = lax.optimization_barrier((jnp.stack(first), jnp.stack(second)))
    return along_z(first) + along_y(second)


def shards(rhs, block_target, pivot_inverse, update_factor, root_inverse, update_map):
    rows = lax.axis_size("row")
    cols = lax.axis_size("col")
    chips = cols // CORES
    half = update_map.shape[0]
    arrived = exchange(pack(rhs, block_target, update_map, rows), "row")
    send, direct, words = route(arrived, rows, half, chips)
    pivot = exchange(send.reshape(rows, half, TILES, SUB, LANES), "row")
    solved, update = front(pivot, pivot_inverse, update_factor)
    returned = exchange(update, "row")
    piece = reduce_cols(*subtract(words, returned, direct, chips), cols)
    pieces = gather_rows(piece, rows, math.isqrt(rows))
    root_solution = reduce_cols(*root(pieces, root_inverse, rows, chips), cols)
    return (solved, root_solution)


def solution(mesh):
    return jax.shard_map(
        shards,
        mesh=mesh,
        in_specs=(
            P(("row", "col"), None),
            P(("row", "col")),
            P(("row", "col"), None),
            P(("row", "col"), None),
            P("row", "col"),
            P(("row", "col")),
        ),
        out_specs=(P(("row", "col"), None), P(("row", "col"), None)),
        check_vma=False,
    )
```
